128 devices in a mesh: gx: 16 (over z, y), gy: 8 (over x, core).
Axes of the slice: x: 4, y: 4, z: 4, core: 2. Of those that a mesh axis runs over, the one named last changes fastest.
Arguments:
- cell_state: float32 [17, 128, 128, 256], P(None, 'gx', 'gy')
- evap_rate: float32 [8], replicated, may hold values from 0.05 to 0.5
- parcels: float32 [8, 2097152], P(None, ('gx', 'gy'))
- crossing: int32 [2, 131072], P(None, ('gx', 'gy')), may hold values from 0 to 16383, as said below
- conv_mass: float32 [8, 262144], P(None, ('gx', 'gy')), may hold values from 0.5 to 2
- conv_owner: int32 [262144, 1], P(('gx', 'gy')), may hold values from 0 to 127; in each aligned block of 2048 rows (0 to 2047, 2048 to 4095, ...) at most 32 rows name the same one
- conv_cell: int32 [262144], P(('gx', 'gy')), may hold values from 0 to 32767
Outputs:
- new_cells: float32 [14, 128, 128, 256], P(None, 'gx', 'gy')
- new_parcels: float32 [8, 2097152], P(None, ('gx', 'gy'))
The draws below stay inside these ranges and needn't reach their ends.
Inputs may be any that keep to these rules, and one draw needn't show every extreme that they name: On each device the 2048 entries of crossing are distinct local parcel slots. `conv_owner`: the rows of one device name one owner at most 32 times.
All inputs are finite; a program needn't handle non-finite values.
Results may differ from the reference program's by a relative error of at most 0.0003.
Values sent between devices are 32-bit elements; how exact they have to be, the bound alone decides.
A program may use at most 64 MiB of HBM per device.

```python
import math
import jax
import jax.numpy as jnp
import numpy as np

SECTIONS = 8
SPECIES = 6
ATTRS = 8
CX = 8
CY = 16
CZ = 256
PAR_DEV = 16384
CONV_DEV = 2048
OWNERS = 128
CROSS = 1024
CAP = 32
CELLS_DEV = 32768
NX = 128
NY = 128
NZ = 256
PARCELS = 2097152
CONV_ROWS = 262144
N_GX = 16
N_GY = 8


def draw_cell_state(key, part):
    key_sec, key_spe, key_vel = jax.random.split(key, 3)
    grid = (NX, NY, NZ)
    sections = jnp.exp(jax.random.uniform(key_sec, (SECTIONS,) + grid, jnp.float32, math.log(0.2), math.log(2.0)))
    species = jax.random.uniform(key_spe, (SPECIES,) + grid, jnp.float32, 0.1, 1.0)
    courant = jax.random.uniform(key_vel, (3,) + grid, jnp.float32, -0.15, 0.15)
    return jnp.concatenate([sections, species, courant], axis=0).astype(jnp.float32)


def draw_parcels(key, part):
    key_pos, key_vel, key_dia, key_tem = jax.random.split(key, 4)
    position = jax.random.normal(key_pos, (3, PARCELS), jnp.float32)
    velocity = jax.random.normal(key_vel, (3, PARCELS), jnp.float32)
    diameter = jax.random.uniform(key_dia, (1, PARCELS), jnp.float32, 0.5, 2.0)
    warmth = jax.random.uniform(key_tem, (1, PARCELS), jnp.float32, 0.5, 1.5)
    return jnp.concatenate([position, velocity, diameter, warmth], axis=0).astype(jnp.float32)


def draw_crossing(key, part):
    device_count = PARCELS // PAR_DEV
    keys = jax.random.split(jax.random.fold_in(key, 17), device_count)
    chosen = jax.vmap(lambda one_key: jax.random.permutation(one_key, PAR_DEV)[:2 * CROSS])(keys)
    chosen = chosen.reshape(device_count, 2, CROSS).transpose(1, 0, 2).reshape(2, device_count * CROSS)
    return chosen.astype(jnp.int32)


def with_ends(values, own_key, least, top_value):
    longest = values.shape.index(max(values.shape))
    spots = []
    for shift in (0, 1):
        where = [jax.random.randint(jax.random.fold_in(own_key, axis), (), 0, length) for axis, length in enumerate(values.shape)]
        where[longest] = (where[longest] + shift) % values.shape[longest]
        spots.append(tuple(where))
    return values.at[spots[0]].set(least).at[spots[1]].set(top_value)


def levels(own_key, dims, shards, smallest, high):
    def one(axis_at, blocks):
        heights = jax.random.uniform(jax.random.fold_in(jax.random.fold_in(own_key, 6), axis_at), (blocks,), jnp.float32, smallest / len(shards), high / len(shards))
        return jnp.repeat(jnp.exp(heights), dims[axis_at] // blocks).reshape((-1,) + (1,) * (len(dims) - axis_at - 1))

    factor_of = one(*shards[0])
    for cut in shards[1:]:
        factor_of = factor_of * one(*cut)
    return factor_of


def routed_block(rng, own, number, rows, count, top, bound, skew):
    ranking = jax.random.permutation(rng, count)
    heavy_load, common = load_shares(count, rows * top, bound, skew, True), load_shares(count, rows * top, bound, skew, False)
    places = jnp.arange(count)

    def named(sizes, offset_by):
        used = int((sizes > 0).sum())
        fixed = max(1, used // 4)
        moved = fixed + (places - fixed + offset_by * (used - fixed)) % max(1, count - fixed)
        return jnp.zeros((count,), jnp.int32).at[ranking[jnp.where(places < fixed, places, moved)]].set(jnp.asarray(sizes, jnp.int32))

    sizes = jnp.where(number % 4 == 0, named(heavy_load, number // 4), named(common, number - number // 4 - 1))
    mixed = jax.random.permutation(jax.random.fold_in(own, 3), count)
    source_of, sink = mixed[0:count // 2 * 2:2], mixed[1:count // 2 * 2:2]
    margin = jnp.minimum(sizes[source_of] - 1, bound - sizes[sink]) // 2
    margin = jnp.where((source_of == ranking[0]) | (sink == ranking[0]) | (sizes[sink] == 0), 0, jnp.maximum(margin, 0))
    moved = jax.random.randint(jax.random.fold_in(own, 4), (count // 2,), 0, 1 << 20) % (margin + 1)
    sizes = sizes.at[source_of].add(-moved).at[sink].add(moved)
    items = jnp.searchsorted(jnp.cumsum(sizes), jnp.arange(rows * top), side="right").astype(jnp.int32)
    table = items.reshape(top, rows).T
    table = table[jax.random.permutation(jax.random.fold_in(own, 1), rows)]
    offset_by = jax.random.randint(jax.random.fold_in(own, 2), (rows, 1), 0, top)
    return jnp.take_along_axis(table, (jnp.arange(top)[None, :] + offset_by) % top, axis=1)


def load_shares(count, total, reach, skew, full):
    portions = [(1 << 20) // math.isqrt(grade ** skew) + 1 for grade in range(1, count + 1)]
    largest = reach if full else min(reach, max(-(-total // count), total * portions[0] // sum(portions)))
    least = 1 if total - largest >= count - 1 else 0
    holding, rest = [largest] + [least] * (count - 1), total - largest - least * (count - 1)
    while rest > 0:
        candidates = [i for i in range(1, count) if holding[i] < largest] or [i for i in range(1, count) if holding[i] < reach]
        whole, left = sum([portions[i] for i in candidates]), rest
        for i in candidates:
            extra = min(reach - holding[i], max(1, left * portions[i] // whole), rest)
            holding[i] = holding[i] + extra
            rest = rest - extra
    return np.array(holding)


def setup_inputs(seed: int = 0) -> dict:
    key_list = jax.random.split(jax.random.key(seed), 8)
    cell_state = draw_cell_state(jax.random.fold_in(key_list[7], 71), 0)
    evap_rate = jnp.clip(jnp.exp(jax.random.uniform(key_list[1], (SECTIONS,), jnp.float32, math.log(0.05), math.log(0.5))), 0.05, 0.5)
    parcels = draw_parcels(jax.random.fold_in(key_list[7], 71), 0)
    crossing = draw_crossing(jax.random.fold_in(key_list[7], 71), 0)
    conv_mass = jnp.clip(jnp.exp(math.log(2.0) - 1.3862944 * jax.random.uniform(key_list[4], (SECTIONS, CONV_ROWS), jnp.float32) ** levels(key_list[4], (SECTIONS, CONV_ROWS), ((1, 128),), -0.2, 0.2)), 0.5, 2.0)
    conv_owner_keys = jax.random.split(jax.random.fold_in(key_list[5], 1), CONV_ROWS // CONV_DEV)
    conv_owner_turns = jax.random.permutation(jax.random.fold_in(key_list[5], 3), CONV_ROWS // CONV_DEV)
    conv_owner = jax.vmap(lambda own, number: routed_block(jax.random.fold_in(key_list[5], 2), own, number, CONV_DEV, OWNERS, 1, CAP, 2))(conv_owner_keys, conv_owner_turns).reshape((CONV_ROWS, 1))
    conv_cell = with_ends(jax.random.randint(key_list[6], (CONV_ROWS,), 0, CELLS_DEV), jax.random.fold_in(key_list[6], 1), 0, CELLS_DEV - 1).astype(jnp.int32)
    return {"cell_state": cell_state, "evap_rate": evap_rate, "parcels": parcels, "crossing": crossing, "conv_mass": conv_mass, "conv_owner": conv_owner, "conv_cell": conv_cell}


def advect(cell_state):
    amount = cell_state[:SECTIONS + SPECIES]
    courant = cell_state[SECTIONS + SPECIES:]
    face_x = 0.5 * (courant[0] + jnp.roll(courant[0], -1, axis=0))
    flux_x = jnp.maximum(face_x, 0.0) * amount + jnp.minimum(face_x, 0.0) * jnp.roll(amount, -1, axis=1)
    change_x = flux_x - jnp.roll(flux_x, 1, axis=1)
    face_y = 0.5 * (courant[1] + jnp.roll(courant[1], -1, axis=1))
    flux_y = jnp.maximum(face_y, 0.0) * amount + jnp.minimum(face_y, 0.0) * jnp.roll(amount, -1, axis=2)
    change_y = flux_y - jnp.roll(flux_y, 1, axis=2)
    face_z = 0.5 * (courant[2][:, :, :-1] + courant[2][:, :, 1:])
    flux_z = jnp.maximum(face_z, 0.0) * amount[:, :, :, :-1] + jnp.minimum(face_z, 0.0) * amount[:, :, :, 1:]
    flux_z = jnp.pad(flux_z, ((0, 0), (0, 0), (0, 0), (1, 1)))
    change_z = flux_z[:, :, :, 1:] - flux_z[:, :, :, :-1]
    return amount - change_x - change_y - change_z


def evaporate(moved, evap_rate):
    sections = moved[:SECTIONS]
    species = moved[SECTIONS:]
    vapour = species[0]
    loss = evap_rate[:, None, None, None] * sections / (1.0 + vapour)
    passed = jnp.concatenate([loss[1:], jnp.zeros_like(loss[:1])], axis=0)
    new_sections = sections - loss + 0.5 * passed
    new_fuel = vapour + loss[0] + 0.5 * jnp.sum(loss[1:], axis=0)
    new_species = jnp.concatenate([new_fuel[None], species[1:]], axis=0)
    return new_sections, new_species


def advance(parcels):
    position = parcels[0:3]
    velocity = parcels[3:6]
    diameter = parcels[6]
    warmth = parcels[7]
    factor = 0.8 / (1.0 + diameter * diameter)
    velocity_new = velocity * (1.0 - factor)
    position_new = position + 0.5 * (velocity + velocity_new)
    diameter_new = diameter * (1.0 - 0.05 * warmth)
    warmth_new = warmth + factor * (1.0 - warmth)
    return jnp.concatenate([position_new, velocity_new, diameter_new[None], warmth_new[None]], axis=0)


def reference(cell_state, evap_rate, parcels, crossing, conv_mass, conv_owner, conv_cell):
    moved = advect(cell_state)
    new_sections, new_species = evaporate(moved, evap_rate)
    owner = conv_owner[:, 0]
    owner_x = owner // N_GY
    owner_y = owner % N_GY
    local_x = conv_cell // (CY * CZ)
    local_y = (conv_cell // CZ) % CY
    local_z = conv_cell % CZ
    flat_cell = ((owner_x * CX + local_x) * NY + owner_y * CY + local_y) * NZ + local_z
    deposit = jnp.zeros((SECTIONS, NX * NY * NZ), jnp.float32).at[:, flat_cell.astype(jnp.int32)].add(conv_mass)
    deposit = deposit.reshape(SECTIONS, NX, NY, NZ)
    new_cells = jnp.concatenate([new_sections + deposit, new_species], axis=0)

    advanced = advance(parcels)
    grouped = advanced.reshape(ATTRS, N_GX, N_GY, PAR_DEV)
    lists = crossing.reshape(2, N_GX, N_GY, CROSS)
    up_sent = jnp.take_along_axis(grouped, jnp.broadcast_to(lists[0][None], (ATTRS, N_GX, N_GY, CROSS)), axis=3)
    down_sent = jnp.take_along_axis(grouped, jnp.broadcast_to(lists[1][None], (ATTRS, N_GX, N_GY, CROSS)), axis=3)
    arrive_up = jnp.roll(up_sent, 1, axis=1)
    arrive_down = jnp.roll(down_sent, -1, axis=1)
    device_base = (jnp.arange(N_GX * N_GY, dtype=jnp.int32) * PAR_DEV).reshape(N_GX, N_GY, 1)
    flat_up = (device_base + lists[0]).reshape(-1).astype(jnp.int32)
    flat_down = (device_base + lists[1]).reshape(-1).astype(jnp.int32)
    new_parcels = advanced.at[:, flat_up].set(arrive_up.reshape(ATTRS, -1))
    new_parcels = new_parcels.at[:, flat_down].set(arrive_down.reshape(ATTRS, -1))
    return new_cells, new_parcels
```

```python
import functools

import jax
import jax.numpy as jnp
from jax import lax
from jax.experimental import pallas as pl
from jax.experimental.pallas import tpu as pltpu
from jax.sharding import PartitionSpec as P

SECTIONS = 8
SPECIES = 6
AMOUNTS = SECTIONS + SPECIES
MESH = pl.DeviceIdType.MESH
F32 = jnp.float32
BF16 = jnp.bfloat16


def split(value):
    high = value.astype(BF16)
    low = (value - high.astype(F32)).astype(BF16)
    return high, low


def dot_nt(left, right):
    return lax.dot_general(left, right, (((1,), (1,)), ((), ())), preferred_element_type=F32)


def iota(shape, dim):
    return lax.broadcasted_iota(jnp.int32, shape, dim)


def step_kernel(
    n_gx, n_gy, cap,
    cell_hbm, evap, par_hbm, cross_hbm, mass_hbm, owner_hbm, landing_hbm,
    out_cells, out_par,
    cell, par, cross, mass, owner, landing,
    hot_owner, slot_vals, packed, packed_own, inbox_y, turned, inbox_x,
    rows_t, hot_plane, hot_depth, spread,
    edge_y, halo_x, halo_y, coef, moved,
    advanced, adv_split, hot_low, leaving, arriving, placing,
    load_sems, s1_send, s1_recv, s2_send, s2_recv, hx_send, hx_recv, hy_send, hy_recv, p_send, p_recv,
):
    gx = lax.axis_index("gx")
    gy = lax.axis_index("gy")
    next_x = lax.rem(gx + 1, n_gx)
    prev_x = lax.rem(gx + n_gx - 1, n_gx)
    next_y = lax.rem(gy + 1, n_gy)
    prev_y = lax.rem(gy + n_gy - 1, n_gy)
    owners = n_gx * n_gy
    rows = mass.shape[1]
    size_x, size_y, size_z = cell.shape[1:]

    loads = [
        pltpu.make_async_copy(src, dst, load_sems.at[i])
        for i, (src, dst) in enumerate((
            (owner_hbm, owner), (mass_hbm, mass), (landing_hbm, landing),
            (cell_hbm, cell), (cross_hbm, cross), (par_hbm, par),
        ))
    ]
    for load in loads:
        load.start()

    barrier = pltpu.get_barrier_semaphore()
    for shift in range(1, n_gx):
        pl.semaphore_signal(barrier, inc=1, device_id=(lax.rem(gx + shift, n_gx), gy), device_id_type=MESH)
    for shift in range(1, n_gy):
        pl.semaphore_signal(barrier, inc=1, device_id=(gx, lax.rem(gy + shift, n_gy)), device_id_type=MESH)

    loads[0].wait()
    loads[1].wait()
    loads[2].wait()
    own = owner[...]
    own = lax.rem(own, n_gy) * n_gx + lax.div(own, n_gy)
    block = 256
    upper = (iota((block, block), 0) < iota((block, block), 1)).astype(F32).astype(BF16)
    count = jnp.zeros((owners, 1), F32)
    for b in range(rows // block):
        at = slice(b * block, (b + 1) * block)
        hot = (iota((owners, block), 0) == own[:, at]).astype(F32)
        hot_b = hot.astype(BF16)
        hot_owner[:, at] = hot_b
        before = jnp.dot(hot_b, upper, preferred_element_type=F32) + count
        rank = jnp.sum(hot * before, axis=0, keepdims=True).astype(jnp.int32)
        count = before[:, block - 1:] + hot[:, block - 1:]
        hot_slot = (iota((cap, block), 0) == rank).astype(F32)
        for s in range(SECTIONS):
            row = mass[s:s + 1, at]
            high = row.astype(BF16).astype(F32)
            slot_vals[0, s * cap:(s + 1) * cap, at] = (hot_slot * high).astype(BF16)
            slot_vals[1, s * cap:(s + 1) * cap, at] = (hot_slot * (row - high)).astype(BF16)
        where_to = landing[:, at]
        depth = lax.rem(where_to, 256)
        slot_vals[0, SECTIONS * cap:(SECTIONS + 1) * cap, at] = (hot_slot * (where_to - depth).astype(F32)).astype(BF16)
        slot_vals[1, SECTIONS * cap:(SECTIONS + 1) * cap, at] = (hot_slot * depth.astype(F32)).astype(BF16)
        slot_vals[0, (SECTIONS + 1) * cap:, at] = jnp.zeros((3 * cap, block), BF16)
        slot_vals[1, (SECTIONS + 1) * cap:, at] = jnp.zeros((3 * cap, block), BF16)
    filled = dot_nt(hot_owner[...], slot_vals[0]) + dot_nt(hot_owner[...], slot_vals[1])
    packed[...] = filled.reshape(n_gy, n_gx, 12 * cap)

    loads[3].wait()
    for f in range(AMOUNTS + 1):
        src = f if f < AMOUNTS else AMOUNTS + 1
        edge_y[0, f] = cell[src, :, 0, :]
        edge_y[1, f] = cell[src, :, size_y - 1, :]

    pl.semaphore_wait(barrier, n_gx + n_gy - 2)

    first = []
    for shift in range(1, n_gy):
        to = lax.rem(gy + shift, n_gy)
        copy = pltpu.make_async_remote_copy(
            packed.at[to], inbox_y.at[gy], s1_send.at[to], s1_recv.at[gy],
            device_id=(gx, to), device_id_type=MESH)
        copy.start()
        first.append(copy)
    halos = []
    for side, plane, to in ((0, size_x - 1, next_x), (1, 0, prev_x)):
        copy = pltpu.make_async_remote_copy(
            cell.at[0:AMOUNTS + 1, plane], halo_x.at[side], hx_send.at[side], hx_recv.at[side],
            device_id=(to, gy), device_id_type=MESH)
        copy.start()
        halos.append(copy)
    for side, edge, to in ((0, 1, next_y), (1, 0, prev_y)):
        copy = pltpu.make_async_remote_copy(
            edge_y.at[edge], halo_y.at[side], hy_send.at[side], hy_recv.at[side],
            device_id=(gx, to), device_id_type=MESH)
        copy.start()
        halos.append(copy)
    inbox_y[gy] = packed[gy]

    loads[4].wait()
    loads[5].wait()
    wide = adv_split.shape[2]
    chunks = par.shape[1] // wide
    attr = iota((8, wide), 0)
    for h in range(chunks):
        at = slice(h * wide, (h + 1) * wide)
        now = par[:, at]
        diameter = now[6:7]
        warmth = now[7:8]
        factor = 0.8 / (1.0 + diameter * diameter)
        keep = 1.0 - factor
        velocity = pltpu.roll(now, 5, 0)
        position_new = now + 0.5 * (velocity + velocity * keep)
        value = jnp.where(
            attr < 3, position_new,
            jnp.where(attr < 6, now * keep,
                      jnp.where(attr < 7, now * (1.0 - 0.05 * warmth), now + factor * (1.0 - now))))
        advanced[:, at] = value
        high = value.astype(BF16)
        both = jnp.concatenate([high.astype(F32), value - high.astype(F32)], axis=0)
        adv_split[h] = both.astype(BF16)
    slots = jnp.concatenate([cross[0:1], cross[1:2]], axis=1)
    total = slots.shape[1]
    low = lax.rem(slots, wide)
    high_part = lax.div(slots, wide)
    part = 256
    for b in range(total // part):
        at = slice(b * part, (b + 1) * part)
        hot_low[:, at] = (iota((wide, part), 0) == low[:, at]).astype(F32).astype(BF16)
    for b in range(total // part):
        at = slice(b * part, (b + 1) * part)
        picked = jnp.dot(adv_split[...].reshape(chunks * 16, wide), hot_low[:, at], preferred_element_type=F32)
        gathered = jnp.zeros((8, part), F32)
        for h in range(chunks):
            one = picked[h * 16:h * 16 + 8] + picked[h * 16 + 8:h * 16 + 16]
            gathered = jnp.where(high_part[:, at] == h, one, gathered)
        half = total // 2
        leaving[b * part // half, :, (b * part) % half:(b * part) % half + part] = gathered
    crossing = []
    for side, to in ((0, next_x), (1, prev_x)):
        copy = pltpu.make_async_remote_copy(
            leaving.at[side], arriving.at[side], p_send.at[side], p_recv.at[side],
            device_id=(to, gy), device_id_type=MESH)
        copy.start()
        crossing.append(copy)

    for shift in range(1, n_gy):
        src = lax.rem(gy + n_gy - shift, n_gy)
        pltpu.make_async_remote_copy(
            packed.at[src], inbox_y.at[src], s1_send.at[src], s1_recv.at[src],
            device_id=(gx, src), device_id_type=MESH).wait_recv()
    for x in range(n_gx):
        turned[x] = inbox_y[:, x, :]
    second = []
    for shift in range(1, n_gx):
        to = lax.rem(gx + shift, n_gx)
        copy = pltpu.make_async_remote_copy(
            turned.at[to], inbox_x.at[gx], s2_send.at[to], s2_recv.at[gx],
            device_id=(to, gy), device_id_type=MESH)
        copy.start()
        second.append(copy)
    inbox_x[gx] = turned[gx]

    for copy in halos:
        copy.wait_recv()
    row_y = iota((size_y, size_z), 0)
    lane_z = iota((size_y, size_z), 1)
    courant_x, courant_y, courant_z = AMOUNTS, AMOUNTS + 1, AMOUNTS + 2

    def across_y(plane, low_row, high_row):
        before = jnp.where(row_y == 0, low_row, pltpu.roll(plane, 1, 0))
        after = jnp.where(row_y == size_y - 1, high_row, pltpu.roll(plane, size_y - 1, 0))
        return before, after

    for x in range(size_x):
        mid = cell[courant_x, x]
        left = halo_x[0, AMOUNTS] if x == 0 else cell[courant_x, x - 1]
        right = halo_x[1, AMOUNTS] if x == size_x - 1 else cell[courant_x, x + 1]
        lower = 0.5 * (left + mid)
        upper_face = 0.5 * (mid + right)
        center = 1.0 - jnp.maximum(upper_face, 0.0) + jnp.minimum(lower, 0.0)
        coef[1, x] = jnp.maximum(lower, 0.0)
        coef[2, x] = -jnp.minimum(upper_face, 0.0)
        mid = cell[courant_y, x]
        before, after = across_y(mid, halo_y[0, AMOUNTS, x:x + 1], halo_y[1, AMOUNTS, x:x + 1])
        lower = 0.5 * (before + mid)
        upper_face = 0.5 * (mid + after)
        center = center - jnp.maximum(upper_face, 0.0) + jnp.minimum(lower, 0.0)
        coef[3, x] = jnp.maximum(lower, 0.0)
        coef[4, x] = -jnp.minimum(upper_face, 0.0)
        mid = cell[courant_z, x]
        lower = jnp.where(lane_z == 0, 0.0, 0.5 * (pltpu.roll(mid, 1, 1) + mid))
        upper_face = jnp.where(lane_z == size_z - 1, 0.0, 0.5 * (mid + pltpu.roll(mid, size_z - 1, 1)))
        center = center - jnp.maximum(upper_face, 0.0) + jnp.minimum(lower, 0.0)
        coef[5, x] = jnp.maximum(lower, 0.0)
        coef[6, x] = -jnp.minimum(upper_face, 0.0)
        coef[0, x] = center

    def transport(f, unused):
        for x in range(size_x):
            mid = cell[f, x]
            left = halo_x[0, f] if x == 0 else cell[f, x - 1]
            right = halo_x[1, f] if x == size_x - 1 else cell[f, x + 1]
            before, after = across_y(mid, halo_y[0, f, x:x + 1], halo_y[1, f, x:x + 1])
            moved[f, x] = (
                coef[0, x] * mid
                + coef[1, x] * left + coef[2, x] * right
                + coef[3, x] * before + coef[4, x] * after
                + coef[5, x] * pltpu.roll(mid, 1, 1) + coef[6, x] * pltpu.roll(mid, size_z - 1, 1))
        return unused

    lax.fori_loop(0, AMOUNTS, transport, 0)

    def evaporate(x, unused):
        vapour = moved[SECTIONS, x]
        inverse = 1.0 / (1.0 + vapour)
        fuel = vapour
        previous = None
        for s in range(SECTIONS):
            dense = moved[s, x]
            loss = evap[s] * dense * inverse
            fuel = fuel + (loss if s == 0 else 0.5 * loss)
            if s > 0:
                out_cells[s - 1, x] = previous + 0.5 * loss
            previous = dense - loss
        out_cells[SECTIONS - 1, x] = previous
        out_cells[SECTIONS, x] = fuel
        for f in range(SECTIONS + 1, AMOUNTS):
            out_cells[f, x] = moved[f, x]
        return unused

    lax.fori_loop(0, size_x, evaporate, 0)

    for copy in crossing:
        copy.wait_recv()
    for b in range(total // part):
        at = slice(b * part, (b + 1) * part)
        half = total // 2
        value = arriving[b * part // half, :, (b * part) % half:(b * part) % half + part]
        high = value.astype(BF16).astype(F32)
        both = jnp.concatenate([high, value - high], axis=0)
        for h in range(chunks):
            placing[h * 16:(h + 1) * 16, at] = jnp.where(high_part[:, at] == h, both, 0.0).astype(BF16)
        placing[chunks * 16:, at] = (iota((chunks, part), 0) == high_part[:, at]).astype(F32).astype(BF16)
    placed = dot_nt(placing[...], hot_low[...])
    for h in range(chunks):
        at = slice(h * wide, (h + 1) * wide)
        hit = placed[chunks * 16 + h:chunks * 16 + h + 1] > 0.5
        value = placed[h * 16:h * 16 + 8] + placed[h * 16 + 8:h * 16 + 16]
        out_par[:, at] = jnp.where(hit, value, advanced[:, at])

    for shift in range(1, n_gx):
        src = lax.rem(gx + n_gx - shift, n_gx)
        pltpu.make_async_remote_copy(
            turned.at[src], inbox_x.at[src], s2_send.at[src], s2_recv.at[src],
            device_id=(src, gy), device_id_type=MESH).wait_recv()
    for part_at in range(3):
        at = slice(part_at * 128, (part_at + 1) * 128)
        rows_t[at, :] = inbox_x[:, :, at].reshape(owners, 128).T
    landed = rows_t[SECTIONS * cap:(SECTIONS + 1) * cap, :].astype(jnp.int32)
    depth = lax.rem(landed, size_z)
    plane = lax.div(landed, size_z)
    planes = size_x * size_y
    for w in range(cap):
        at = slice(w * owners, (w + 1) * owners)
        hot_plane[:, at] = (iota((planes, owners), 0) == plane[w:w + 1]).astype(F32).astype(BF16)
        hot_depth[:, at] = (iota((size_z, owners), 0) == depth[w:w + 1]).astype(F32).astype(BF16)

    def deposit(s, unused):
        values = rows_t[pl.ds(pl.multiple_of(s * cap, cap), cap), :]
        high = values.astype(BF16).astype(F32)
        low = values - high
        for w in range(cap):
            at = slice(w * owners, (w + 1) * owners)
            hot = hot_plane[:, at].reshape(planes // 16, 16, owners)
            one = jnp.broadcast_to(high[w:w + 1], (16, owners)).astype(BF16)
            spread[0:planes, at] = (hot * one[None]).reshape(planes, owners)
            one = jnp.broadcast_to(low[w:w + 1], (16, owners)).astype(BF16)
            spread[planes:, at] = (hot * one[None]).reshape(planes, owners)
        added = dot_nt(spread[...], hot_depth[...])
        added = added[:planes] + added[planes:]
        out_cells[s] = out_cells[s] + added.reshape(size_x, size_y, size_z)
        return unused

    lax.fori_loop(0, SECTIONS, deposit, 0)

    for copy in first + second + halos + crossing:
        copy.wait_send()


def on_device(cell_state, evap_rate, parcels, crossing, conv_mass, conv_owner, conv_cell, n_gx, n_gy):
    fields, size_x, size_y, size_z = cell_state.shape
    rows = conv_mass.shape[1]
    owners = n_gx * n_gy
    cap = 2 * rows // owners
    slots = parcels.shape[1]
    total = 2 * crossing.shape[1]
    wide = 512
    chunks = slots // wide
    planes = size_x * size_y
    lanes = 12 * cap
    any_spec = pl.BlockSpec(memory_space=pl.ANY)
    dma = pltpu.SemaphoreType.DMA
    vmem = pltpu.VMEM
    return pl.pallas_call(
        functools.partial(step_kernel, n_gx, n_gy, cap),
        out_shape=(
            jax.ShapeDtypeStruct((AMOUNTS, size_x, size_y, size_z), F32),
            jax.ShapeDtypeStruct(parcels.shape, F32),
        ),
        in_specs=[any_spec, pl.BlockSpec(memory_space=pltpu.SMEM)] + [any_spec] * 5,
        out_specs=(pl.BlockSpec(memory_space=pltpu.VMEM), pl.BlockSpec(memory_space=pltpu.VMEM)),
        scratch_shapes=[
            vmem(cell_state.shape, F32), vmem(parcels.shape, F32), vmem(crossing.shape, jnp.int32),
            vmem(conv_mass.shape, F32), vmem((1, rows), jnp.int32), vmem((1, rows), jnp.int32),
            vmem((owners, rows), BF16), vmem((2, lanes, rows), BF16),
            vmem((n_gy, n_gx, lanes), F32), vmem((n_gx, lanes), F32), vmem((n_gy, n_gx, lanes), F32),
            vmem((n_gx, n_gy, lanes), F32), vmem((n_gx, n_gy, lanes), F32),
            vmem((lanes, owners), F32), vmem((planes, cap * owners), BF16),
            vmem((size_z, cap * owners), BF16), vmem((2 * planes, cap * owners), BF16),
            vmem((2, AMOUNTS + 1, size_x, size_z), F32), vmem((2, AMOUNTS + 1, size_y, size_z), F32),
            vmem((2, AMOUNTS + 1, size_x, size_z), F32),
            vmem((7, size_x, size_y, size_z), F32), vmem((AMOUNTS, size_x, size_y, size_z), F32),
            vmem(parcels.shape, F32), vmem((chunks, 16, wide), BF16), vmem((wide, total), BF16),
            vmem((2, 8, total // 2), F32), vmem((2, 8, total // 2), F32), vmem((chunks * 17, total), BF16),
            dma((6,)), dma((n_gy,)), dma((n_gy,)), dma((n_gx,)), dma((n_gx,)),
            dma((2,)), dma((2,)), dma((2,)), dma((2,)), dma((2,)), dma((2,)),
        ],
        compiler_params=pltpu.CompilerParams(
            collective_id=0, has_side_effects=True, vmem_limit_bytes=60 << 20),
        name="spray_step",
    )(
        cell_state, evap_rate, parcels, crossing, conv_mass,
        conv_owner.reshape(1, rows), conv_cell.reshape(1, rows),
    )


def solution(mesh):
    in_specs = (
        P(None, "gx", "gy", None),
        P(),
        P(None, ("gx", "gy")),
        P(None, ("gx", "gy")),
        P(None, ("gx", "gy")),
        P(("gx", "gy"), None),
        P(("gx", "gy")),
    )
    out_specs = (P(None, "gx", "gy", None), P(None, ("gx", "gy")))
    return jax.shard_map(
        functools.partial(on_device, n_gx=mesh.shape["gx"], n_gy=mesh.shape["gy"]),
        mesh=mesh, in_specs=in_specs, out_specs=out_specs, check_vma=False,
    )
```

```python
import functools

import jax
import jax.numpy as jnp
from jax import lax
from jax.experimental import pallas as pl
from jax.experimental.pallas import tpu as pltpu
from jax.sharding import PartitionSpec as P

SECTIONS = 8
SPECIES = 6
AMOUNTS = SECTIONS + SPECIES
MESH = pl.DeviceIdType.MESH
F32 = jnp.float32
BF16 = jnp.bfloat16
F8 = jnp.float8_e4m3fn


def dot_nt(left, right):
    return lax.dot_general(left, right, (((1,), (1,)), ((), ())), preferred_element_type=F32)


def iota(shape, dim):
    return lax.broadcasted_iota(jnp.int32, shape, dim)


def step_kernel(
    n_gx, n_gy, cap,
    cell_hbm, evap, par_hbm, cross_hbm, mass_hbm, owner_hbm, landing_hbm,
    out_cells, out_par, out_rows,
    cell, par, cross, mass, owner, landing,
    hot_owner, slot_vals, packed, packed_own, inbox_y, turned, inbox_x,
    edge_y, halo_x, halo_y, coef, moved,
    advanced, adv_split, hot_low, leaving, arriving, placing,
    load_sems, s1_send, s1_recv, s2_send, s2_recv, hx_send, hx_recv, hy_send, hy_recv, p_send, p_recv,
):
    gx = lax.axis_index("gx")
    gy = lax.axis_index("gy")
    next_x = lax.rem(gx + 1, n_gx)
    prev_x = lax.rem(gx + n_gx - 1, n_gx)
    next_y = lax.rem(gy + 1, n_gy)
    prev_y = lax.rem(gy + n_gy - 1, n_gy)
    owners = n_gx * n_gy
    rows = mass.shape[1]
    size_x, size_y, size_z = cell.shape[1:]

    loads = [
        pltpu.make_async_copy(src, dst, load_sems.at[i])
        for i, (src, dst) in enumerate((
            (owner_hbm, owner), (mass_hbm, mass), (landing_hbm, landing),
            (cell_hbm, cell), (cross_hbm, cross), (par_hbm, par),
        ))
    ]
    for load in loads:
        load.start()

    barrier = pltpu.get_barrier_semaphore()
    for shift in range(1, n_gx):
        pl.semaphore_signal(barrier, inc=1, device_id=(lax.rem(gx + shift, n_gx), gy), device_id_type=MESH)
    for shift in range(1, n_gy):
        pl.semaphore_signal(barrier, inc=1, device_id=(gx, lax.rem(gy + shift, n_gy)), device_id_type=MESH)

    loads[0].wait()
    loads[1].wait()
    loads[2].wait()
    own = owner[...]
    own = lax.rem(own, n_gy) * n_gx + lax.div(own, n_gy)
    block = 256
    upper = (iota((block, block), 0) < iota((block, block), 1)).astype(F32).astype(BF16)
    count = jnp.zeros((owners, 1), F32)
    for b in range(rows // block):
        at = slice(b * block, (b + 1) * block)
        hot = (iota((owners, block), 0) == own[:, at]).astype(F32)
        hot_b = hot.astype(BF16)
        hot_owner[:, at] = hot_b
        before = jnp.dot(hot_b, upper, preferred_element_type=F32) + count
        rank = jnp.sum(hot * before, axis=0, keepdims=True).astype(jnp.int32)
        count = before[:, block - 1:] + hot[:, block - 1:]
        hot_slot = (iota((cap, block), 0) == rank).astype(F32)
        for s in range(SECTIONS):
            row = mass[s:s + 1, at]
            high = row.astype(BF16).astype(F32)
            slot_vals[0, s * cap:(s + 1) * cap, at] = (hot_slot * high).astype(BF16)
            slot_vals[1, s * cap:(s + 1) * cap, at] = (hot_slot * (row - high)).astype(BF16)
        where_to = landing[:, at]
        depth = lax.rem(where_to, 256)
        slot_vals[0, SECTIONS * cap:(SECTIONS + 1) * cap, at] = (hot_slot * (where_to - depth).astype(F32)).astype(BF16)
        slot_vals[1, SECTIONS * cap:(SECTIONS + 1) * cap, at] = (hot_slot * depth.astype(F32)).astype(BF16)
        slot_vals[0, (SECTIONS + 1) * cap:, at] = jnp.zeros((3 * cap, block), BF16)
        slot_vals[1, (SECTIONS + 1) * cap:, at] = jnp.zeros((3 * cap, block), BF16)
    filled = dot_nt(hot_owner[...], slot_vals[0]) + dot_nt(hot_owner[...], slot_vals[1])
    packed[...] = filled.reshape(n_gy, n_gx, 12 * cap)

    loads[3].wait()
    for f in range(AMOUNTS + 1):
        src = f if f < AMOUNTS else AMOUNTS + 1
        edge_y[0, f] = cell[src, :, 0, :]
        edge_y[1, f] = cell[src, :, size_y - 1, :]

    pl.semaphore_wait(barrier, n_gx + n_gy - 2)

    first = []
    for shift in range(1, n_gy):
        to = lax.rem(gy + shift, n_gy)
        copy = pltpu.make_async_remote_copy(
            packed.at[to], inbox_y.at[gy], s1_send.at[to], s1_recv.at[gy],
            device_id=(gx, to), device_id_type=MESH)
        copy.start()
        first.append(copy)
    halos = []
    for side, plane, to in ((0, size_x - 1, next_x), (1, 0, prev_x)):
        copy = pltpu.make_async_remote_copy(
            cell.at[0:AMOUNTS + 1, plane], halo_x.at[side], hx_send.at[side], hx_recv.at[side],
            device_id=(to, gy), device_id_type=MESH)
        copy.start()
        halos.append(copy)
    for side, edge, to in ((0, 1, next_y), (1, 0, prev_y)):
        copy = pltpu.make_async_remote_copy(
            edge_y.at[edge], halo_y.at[side], hy_send.at[side], hy_recv.at[side],
            device_id=(gx, to), device_id_type=MESH)
        copy.start()
        halos.append(copy)
    inbox_y[gy] = packed[gy]

    loads[4].wait()
    loads[5].wait()
    wide = adv_split.shape[2]
    chunks = par.shape[1] // wide
    attr = iota((8, wide), 0)
    for h in range(chunks):
        at = slice(h * wide, (h + 1) * wide)
        now = par[:, at]
        diameter = now[6:7]
        warmth = now[7:8]
        factor = 0.8 / (1.0 + diameter * diameter)
        keep = 1.0 - factor
        velocity = pltpu.roll(now, 5, 0)
        position_new = now + 0.5 * (velocity + velocity * keep)
        value = jnp.where(
            attr < 3, position_new,
            jnp.where(attr < 6, now * keep,
                      jnp.where(attr < 7, now * (1.0 - 0.05 * warmth), now + factor * (1.0 - now))))
        advanced[:, at] = value
        high = value.astype(BF16)
        both = jnp.concatenate([high.astype(F32), value - high.astype(F32)], axis=0)
        adv_split[h] = both.astype(BF16)
    slots = jnp.concatenate([cross[0:1], cross[1:2]], axis=1)
    total = slots.shape[1]
    low = lax.rem(slots, wide)
    high_part = lax.div(slots, wide)
    part = 256
    for b in range(total // part):
        at = slice(b * part, (b + 1) * part)
        hot_low[:, at] = (iota((wide, part), 0) == low[:, at]).astype(F32).astype(BF16)
    for b in range(total // part):
        at = slice(b * part, (b + 1) * part)
        picked = jnp.dot(adv_split[...].reshape(chunks * 16, wide), hot_low[:, at], preferred_element_type=F32)
        gathered = jnp.zeros((8, part), F32)
        for h in range(chunks):
            one = picked[h * 16:h * 16 + 8] + picked[h * 16 + 8:h * 16 + 16]
            gathered = jnp.where(high_part[:, at] == h, one, gathered)
        half = total // 2
        leaving[b * part // half, :, (b * part) % half:(b * part) % half + part] = gathered
    crossing = []
    for side, to in ((0, next_x), (1, prev_x)):
        copy = pltpu.make_async_remote_copy(
            leaving.at[side], arriving.at[side], p_send.at[side], p_recv.at[side],
            device_id=(to, gy), device_id_type=MESH)
        copy.start()
        crossing.append(copy)

    for shift in range(1, n_gy):
        src = lax.rem(gy + n_gy - shift, n_gy)
        pltpu.make_async_remote_copy(
            packed.at[src], inbox_y.at[src], s1_send.at[src], s1_recv.at[src],
            device_id=(gx, src), device_id_type=MESH).wait_recv()
    for x in range(n_gx):
        turned[x] = inbox_y[:, x, :]
    second = []
    for shift in range(1, n_gx):
        to = lax.rem(gx + shift, n_gx)
        copy = pltpu.make_async_remote_copy(
            turned.at[to], inbox_x.at[gx], s2_send.at[to], s2_recv.at[gx],
            device_id=(to, gy), device_id_type=MESH)
        copy.start()
        second.append(copy)
    inbox_x[gx] = turned[gx]

    for copy in halos:
        copy.wait_recv()
    row_y = iota((size_y, size_z), 0)
    lane_z = iota((size_y, size_z), 1)
    courant_x, courant_y, courant_z = AMOUNTS, AMOUNTS + 1, AMOUNTS + 2

    def across_y(plane, low_row, high_row):
        before = jnp.where(row_y == 0, low_row, pltpu.roll(plane, 1, 0))
        after = jnp.where(row_y == size_y - 1, high_row, pltpu.roll(plane, size_y - 1, 0))
        return before, after

    for x in range(size_x):
        mid = cell[courant_x, x]
        left = halo_x[0, AMOUNTS] if x == 0 else cell[courant_x, x - 1]
        right = halo_x[1, AMOUNTS] if x == size_x - 1 else cell[courant_x, x + 1]
        lower = 0.5 * (left + mid)
        upper_face = 0.5 * (mid + right)
        center = 1.0 - jnp.maximum(upper_face, 0.0) + jnp.minimum(lower, 0.0)
        coef[1, x] = jnp.maximum(lower, 0.0)
        coef[2, x] = -jnp.minimum(upper_face, 0.0)
        mid = cell[courant_y, x]
        before, after = across_y(mid, halo_y[0, AMOUNTS, x:x + 1], halo_y[1, AMOUNTS, x:x + 1])
        lower = 0.5 * (before + mid)
        upper_face = 0.5 * (mid + after)
        center = center - jnp.maximum(upper_face, 0.0) + jnp.minimum(lower, 0.0)
        coef[3, x] = jnp.maximum(lower, 0.0)
        coef[4, x] = -jnp.minimum(upper_face, 0.0)
        mid = cell[courant_z, x]
        lower = jnp.where(lane_z == 0, 0.0, 0.5 * (pltpu.roll(mid, 1, 1) + mid))
        upper_face = jnp.where(lane_z == size_z - 1, 0.0, 0.5 * (mid + pltpu.roll(mid, size_z - 1, 1)))
        center = center - jnp.maximum(upper_face, 0.0) + jnp.minimum(lower, 0.0)
        coef[5, x] = jnp.maximum(lower, 0.0)
        coef[6, x] = -jnp.minimum(upper_face, 0.0)
        coef[0, x] = center

    def transport(f, unused):
        for x in range(size_x):
            mid = cell[f, x]
            left = halo_x[0, f] if x == 0 else cell[f, x - 1]
            right = halo_x[1, f] if x == size_x - 1 else cell[f, x + 1]
            before, after = across_y(mid, halo_y[0, f, x:x + 1], halo_y[1, f, x:x + 1])
            moved[f, x] = (
                coef[0, x] * mid
                + coef[1, x] * left + coef[2, x] * right
                + coef[3, x] * before + coef[4, x] * after
                + coef[5, x] * pltpu.roll(mid, 1, 1) + coef[6, x] * pltpu.roll(mid, size_z - 1, 1))
        return unused

    lax.fori_loop(0, AMOUNTS, transport, 0)

    def evaporate(x, unused):
        vapour = moved[SECTIONS, x]
        inverse = 1.0 / (1.0 + vapour)
        fuel = vapour
        previous = None
        for s in range(SECTIONS):
            dense = moved[s, x]
            loss = evap[s] * dense * inverse
            fuel = fuel + (loss if s == 0 else 0.5 * loss)
            if s > 0:
                out_cells[s - 1, x] = previous + 0.5 * loss
            previous = dense - loss
        out_cells[SECTIONS - 1, x] = previous
        out_cells[SECTIONS, x] = fuel
        for f in range(SECTIONS + 1, AMOUNTS):
            out_cells[f, x] = moved[f, x]
        return unused

    lax.fori_loop(0, size_x, evaporate, 0)

    for copy in crossing:
        copy.wait_recv()
    for b in range(total // part):
        at = slice(b * part, (b + 1) * part)
        half = total // 2
        value = arriving[b * part // half, :, (b * part) % half:(b * part) % half + part]
        high = value.astype(BF16).astype(F32)
        both = jnp.concatenate([high, value - high], axis=0)
        for h in range(chunks):
            placing[h * 16:(h + 1) * 16, at] = jnp.where(high_part[:, at] == h, both, 0.0).astype(BF16)
        placing[chunks * 16:, at] = (iota((chunks, part), 0) == high_part[:, at]).astype(F32).astype(BF16)
    placed = dot_nt(placing[...], hot_low[...])
    for h in range(chunks):
        at = slice(h * wide, (h + 1) * wide)
        hit = placed[chunks * 16 + h:chunks * 16 + h + 1] > 0.5
        value = placed[h * 16:h * 16 + 8] + placed[h * 16 + 8:h * 16 + 16]
        out_par[:, at] = jnp.where(hit, value, advanced[:, at])

    for shift in range(1, n_gx):
        src = lax.rem(gx + n_gx - shift, n_gx)
        pltpu.make_async_remote_copy(
            turned.at[src], inbox_x.at[src], s2_send.at[src], s2_recv.at[src],
            device_id=(src, gy), device_id_type=MESH).wait_recv()
    out_rows[...] = inbox_x[...]
    for copy in first + second + halos + crossing:
        copy.wait_send()


def deposit_kernel(
    cap, landed, cells, parcels, out_cells, out_par,
    sums, rows_t, hot_plane, hot_depth, spread, sems,
):
    lasting = [pltpu.make_async_copy(parcels, out_par, sems.at[AMOUNTS])]
    for f in range(SECTIONS, AMOUNTS):
        lasting.append(pltpu.make_async_copy(cells.at[f], out_cells.at[f], sems.at[f]))
    for copy in lasting:
        copy.start()
    size_x, size_y, size_z = cells.shape[1:]
    planes = size_x * size_y
    n_gx, n_gy = landed.shape[:2]
    owners = n_gx * n_gy
    for part in range(3):
        at = slice(part * 128, (part + 1) * 128)
        rows_t[at, :] = landed[:, :, at].reshape(owners, 128).T
    plane = lax.div(rows_t[SECTIONS * cap:(SECTIONS + 1) * cap, :].astype(jnp.int32), size_z)
    depth = lax.rem(landed[:, :, SECTIONS * cap:].reshape(owners, 4 * cap).astype(jnp.int32), size_z)
    for w in range(cap):
        at = slice(w * owners, (w + 1) * owners)
        hot_plane[:, at] = (iota((planes, owners), 0) == plane[w:w + 1]).astype(F32).astype(BF16)
        hot_depth[at, :] = (iota((owners, size_z), 1) == depth[:, w:w + 1]).astype(F32).astype(F8)

    def deposit(s, unused):
        values = rows_t[pl.ds(pl.multiple_of(s * cap, cap), cap), :]
        first = values.astype(F8).astype(F32)
        rest = (values - first) * 16.0
        second = rest.astype(F8).astype(F32)
        third = (rest - second) * 16.0
        for w in range(cap):
            at = slice(w * owners, (w + 1) * owners)
            hot = hot_plane[:, at].reshape(planes // 16, 16, owners)
            for p, piece in enumerate((first, second, third)):
                one = jnp.broadcast_to(piece[w:w + 1], (16, owners)).astype(BF16)
                spread[p * planes:(p + 1) * planes, at] = (hot * one[None]).reshape(planes, owners).astype(F8)
        added = jnp.dot(spread[...], hot_depth[...], preferred_element_type=F32)
        added = added[:planes] + added[planes:2 * planes] * (1 / 16) + added[2 * planes:] * (1 / 256)
        sums[s] = cells[s] + added.reshape(size_x, size_y, size_z)
        pltpu.make_async_copy(sums.at[s], out_cells.at[s], sems.at[s]).start()
        return unused

    lax.fori_loop(0, SECTIONS, deposit, 0)
    for s in range(SECTIONS):
        pltpu.make_async_copy(sums.at[s], out_cells.at[s], sems.at[s]).wait()
    for copy in lasting:
        copy.wait()


def on_device(cell_state, evap_rate, parcels, crossing, conv_mass, conv_owner, conv_cell, n_gx, n_gy):
    fields, size_x, size_y, size_z = cell_state.shape
    rows = conv_mass.shape[1]
    owners = n_gx * n_gy
    cap = 2 * rows // owners
    slots = parcels.shape[1]
    total = 2 * crossing.shape[1]
    wide = 512
    chunks = slots // wide
    planes = size_x * size_y
    lanes = 12 * cap
    any_spec = pl.BlockSpec(memory_space=pltpu.HBM)
    dma = pltpu.SemaphoreType.DMA
    vmem = pltpu.VMEM
    whole = pl.BlockSpec(memory_space=vmem)
    cells, new_parcels, landed = pl.pallas_call(
        functools.partial(step_kernel, n_gx, n_gy, cap),
        out_shape=(
            vmem((AMOUNTS, size_x, size_y, size_z), F32),
            vmem(parcels.shape, F32),
            vmem((n_gx, n_gy, lanes), F32),
        ),
        in_specs=[any_spec, pl.BlockSpec(memory_space=pltpu.SMEM)] + [any_spec] * 5,
        out_specs=(whole, whole, whole),
        scratch_shapes=[
            vmem(cell_state.shape, F32), vmem(parcels.shape, F32), vmem(crossing.shape, jnp.int32),
            vmem(conv_mass.shape, F32), vmem((1, rows), jnp.int32), vmem((1, rows), jnp.int32),
            vmem((owners, rows), BF16), vmem((2, lanes, rows), BF16),
            vmem((n_gy, n_gx, lanes), F32), vmem((n_gx, lanes), F32), vmem((n_gy, n_gx, lanes), F32),
            vmem((n_gx, n_gy, lanes), F32), vmem((n_gx, n_gy, lanes), F32),
            vmem((2, AMOUNTS + 1, size_x, size_z), F32), vmem((2, AMOUNTS + 1, size_y, size_z), F32),
            vmem((2, AMOUNTS + 1, size_x, size_z), F32),
            vmem((7, size_x, size_y, size_z), F32), vmem((AMOUNTS, size_x, size_y, size_z), F32),
            vmem(parcels.shape, F32), vmem((chunks, 16, wide), BF16), vmem((wide, total), BF16),
            vmem((2, 8, total // 2), F32), vmem((2, 8, total // 2), F32), vmem((chunks * 17, total), BF16),
            dma((6,)), dma((n_gy,)), dma((n_gy,)), dma((n_gx,)), dma((n_gx,)),
            dma((2,)), dma((2,)), dma((2,)), dma((2,)), dma((2,)), dma((2,)),
        ],
        compiler_params=pltpu.CompilerParams(
            collective_id=0, has_side_effects=True, vmem_limit_bytes=61 << 20),
        name="spray_step",
    )(
        cell_state, evap_rate, parcels, crossing, conv_mass,
        conv_owner.reshape(1, rows), conv_cell.reshape(1, rows),
    )
    return pl.pallas_call(
        functools.partial(deposit_kernel, cap),
        out_shape=(
            jax.ShapeDtypeStruct((AMOUNTS, size_x, size_y, size_z), F32),
            jax.ShapeDtypeStruct(parcels.shape, F32),
        ),
        in_specs=[whole] * 3,
        out_specs=(any_spec, any_spec),
        scratch_shapes=[
            vmem((SECTIONS, size_x, size_y, size_z), F32), vmem((lanes, owners), F32),
            vmem((planes, cap * owners), BF16), vmem((cap * owners, size_z), F8),
            vmem((3 * planes, cap * owners), F8), dma((AMOUNTS + 1,)),
        ],
        compiler_params=pltpu.CompilerParams(vmem_limit_bytes=28 << 20),
        name="deposit",
    )(landed, cells, new_parcels)


def solution(mesh):
    in_specs = (
        P(None, "gx", "gy", None),
        P(),
        P(None, ("gx", "gy")),
        P(None, ("gx", "gy")),
        P(None, ("gx", "gy")),
        P(("gx", "gy"), None),
        P(("gx", "gy")),
    )
    out_specs = (P(None, "gx", "gy", None), P(None, ("gx", "gy")))
    return jax.shard_map(
        functools.partial(on_device, n_gx=mesh.shape["gx"], n_gy=mesh.shape["gy"]),
        mesh=mesh, in_specs=in_specs, out_specs=out_specs, check_vma=False,
    )
```
